32 devices in a mesh: lat: 4 (over x, core), lon: 8 (over z, y).
Axes of the slice: x: 2, y: 2, z: 4, core: 2. Of those that a mesh axis runs over, the one named last changes fastest.
Arguments:
- tokens: bfloat16 [64, 128, 1024], P('lat', 'lon'), may hold values from -6 to 6
- norm_gain: float32 [1024], replicated, may hold values from 0.25 to 1.75
- w_qkv: bfloat16 [1024, 3072], replicated, may hold values from -0.1875 to 0.1875
- w_out: bfloat16 [1024, 1024], replicated, may hold values from -0.1875 to 0.1875
- cotangent: bfloat16 [64, 128, 1024], P('lat', 'lon'), may hold values from -6 to 6
Outputs:
- result: bfloat16 [64, 128, 1024], P('lat', 'lon')
- grad_tokens: bfloat16 [64, 128, 1024], P('lat', 'lon')
- grad_w_qkv: float32 [1024, 3072], P(('lat', 'lon'))
- grad_w_out: float32 [1024, 1024], P(('lat', 'lon'))
The draws below stay inside these ranges and needn't reach their ends.
All inputs are finite; a program needn't handle non-finite values.
Results may differ from the reference program's by a relative error of at most 0.025.
Values may be sent and summed in bfloat16 or wider, within the bound.
A program may use at most 192 MiB of HBM per device.

```python
import jax
import jax.numpy as jnp
from jax import lax

D = 1024
H = 16
R = 6
NLAT = 64
NLON = 128


def spiked(entries, stream_key, source, target, shards_of, factor):
    def block_of(dim):
        return (jnp.arange(entries.shape[dim]) // (entries.shape[dim] // shards_of)).reshape((-1,) + (1,) * (entries.ndim - 1 - dim))

    near = jax.random.permutation(stream_key, shards_of)[block_of(target)]
    far = (block_of(target) + shards_of // 2) % shards_of
    return jnp.where((block_of(source) == near) | (block_of(source) == far), factor * entries, entries)


def steps_of(own_key, shape, cuts, smallest, largest):
    def one(dim, blocks):
        heights = jax.random.uniform(jax.random.fold_in(jax.random.fold_in(own_key, 6), dim), (blocks,), jnp.float32, smallest / len(cuts), largest / len(cuts))
        return jnp.repeat(jnp.exp(heights), shape[dim] // blocks).reshape((-1,) + (1,) * (len(shape) - dim - 1))

    loudness = one(*cuts[0])
    for cut in cuts[1:]:
        loudness = loudness * one(*cut)
    return loudness


def centred(stream_key, shape, width, bound, split=(), dtype=jnp.bfloat16):
    drawn = jax.random.normal(stream_key, shape, jnp.float32) * width
    if len(split) > 0:
        drawn = steps_of(stream_key, shape, split, -0.22, 0.18) * drawn
    return jnp.clip(drawn, min=-bound, max=bound).astype(dtype)


def heavy_noise(stream_key, extent, width, reach, pieces, heavy, held_as=jnp.bfloat16):
    values = width * jax.random.normal(stream_key, extent, jnp.float32)
    if pieces:
        values = values * steps_of(stream_key, extent, pieces, -0.22, 0.18)
    return jnp.clip(spiked(values, jax.random.fold_in(stream_key, 3), *heavy), -reach, reach).astype(held_as)


def setup_inputs(seed: int = 0) -> dict:
    arg_keys = jax.random.split(jax.random.key(seed), 6)
    return {
        "tokens": heavy_noise(arg_keys[0], (NLAT, NLON, D), 1.0, 6.0, ((0, 4), (1, 8)), (1, 2, 8, 2.0)),
        "norm_gain": jnp.clip(1.0 + 0.15 * jax.random.normal(arg_keys[1], (D,), jnp.float32), 0.25, 1.75),
        "w_qkv": centred(arg_keys[2], (D, 3 * D), D ** -0.5, 0.1875),
        "w_out": centred(arg_keys[3], (D, D), D ** -0.5, 0.1875),
        "cotangent": centred(arg_keys[4], (NLAT, NLON, D), 1.0, 6.0, ((0, 4), (1, 8))),
    }


epsilon = 1e-06

def extend(values):
    turned = jnp.roll(values, NLON // 2, axis=1)
    north_rows = turned[:R][::-1]
    south_rows = turned[NLAT - R:][::-1]
    stacked = jnp.concatenate([north_rows, values, south_rows], axis=0)
    return jnp.concatenate([stacked[:, NLON - R:], stacked, stacked[:, :R]], axis=1)

def shifted(stripe, offset):
    line = lax.dynamic_index_in_dim(stripe, offset, 0, keepdims=False)
    return jnp.stack([line[column:column + NLON] for column in range(2 * R + 1)])

def heads_of(values):
    return values.astype(jnp.float32).reshape(values.shape[:-1] + (H, D // H))

def rounded(values):
    return lax.optimization_barrier(values.astype(jnp.bfloat16)).astype(jnp.float32)

def offsets_list():
    return jnp.arange(2 * R + 1).astype(jnp.int32)

def forward_row(row_index, queries, keys_ext, values_ext):
    factor = (D // H) ** (-0.5)
    centre = heads_of(queries[row_index])
    key_stripe = lax.dynamic_slice_in_dim(keys_ext, row_index, 2 * R + 1, 0)
    value_stripe = lax.dynamic_slice_in_dim(values_ext, row_index, 2 * R + 1, 0)

    def score_line(offset):
        return jnp.einsum('nhd,bnhd->bnh', centre, heads_of(shifted(key_stripe, offset))) * factor
    scores = lax.map(score_line, offsets_list())
    highest = lax.optimization_barrier(jnp.max(scores, axis=(0, 1)))
    log_total = highest + jnp.log(lax.optimization_barrier(jnp.sum(jnp.exp(scores - highest), axis=(0, 1))))
    chances_low = rounded(jnp.exp(scores - log_total))

    def add_line(summed, inputs):
        offset, weights = inputs
        return (summed + jnp.einsum('bnh,bnhd->nhd', weights, heads_of(shifted(value_stripe, offset))), None)
    initial = jnp.zeros((NLON, H, D // H), jnp.float32)
    summed, unused = lax.scan(add_line, initial, (offsets_list(), chances_low))
    return (summed.reshape(NLON, D).astype(jnp.bfloat16), log_total)

def query_row(row_index, queries, grads, totals, deltas, keys_ext, values_ext):
    factor = (D // H) ** (-0.5)
    centre = heads_of(queries[row_index])
    incoming = heads_of(grads[row_index])
    row_total = totals[row_index]
    row_delta = deltas[row_index]
    key_stripe = lax.dynamic_slice_in_dim(keys_ext, row_index, 2 * R + 1, 0)
    value_stripe = lax.dynamic_slice_in_dim(values_ext, row_index, 2 * R + 1, 0)

    def add_line(summed, offset):
        keys_here = heads_of(shifted(key_stripe, offset))
        values_here = heads_of(shifted(value_stripe, offset))
        scores = jnp.einsum('nhd,bnhd->bnh', centre, keys_here) * factor
        chances = jnp.exp(scores - row_total)
        grad_chances = jnp.einsum('nhd,bnhd->bnh', incoming, values_here)
        grad_scores = rounded(chances * (grad_chances - row_delta))
        return (summed + jnp.einsum('bnh,bnhd->nhd', grad_scores, keys_here), None)
    initial = jnp.zeros((NLON, H, D // H), jnp.float32)
    summed, unused = lax.scan(add_line, initial, offsets_list())
    return (summed * factor).reshape(NLON, D)

def key_row(row_index, keys, values, queries_ext, grads_ext, totals_ext, deltas_ext):
    factor = (D // H) ** (-0.5)
    own_keys = heads_of(keys[row_index])
    own_values = heads_of(values[row_index])
    query_stripe = lax.dynamic_slice_in_dim(queries_ext, row_index, 2 * R + 1, 0)
    grad_stripe = lax.dynamic_slice_in_dim(grads_ext, row_index, 2 * R + 1, 0)
    total_stripe = lax.dynamic_slice_in_dim(totals_ext, row_index, 2 * R + 1, 0)
    delta_stripe = lax.dynamic_slice_in_dim(deltas_ext, row_index, 2 * R + 1, 0)

    def add_line(sums, offset):
        far_queries = heads_of(shifted(query_stripe, offset))
        far_grads = heads_of(shifted(grad_stripe, offset))
        far_totals = shifted(total_stripe, offset)
        far_deltas = shifted(delta_stripe, offset)
        scores = jnp.einsum('nhd,bnhd->bnh', own_keys, far_queries) * factor
        chances = jnp.exp(scores - far_totals)
        grad_chances = jnp.einsum('nhd,bnhd->bnh', own_values, far_grads)
        grad_scores = rounded(chances * (grad_chances - far_deltas))
        chances_low = rounded(chances)
        key_sum = sums[0] + jnp.einsum('bnh,bnhd->nhd', grad_scores, far_queries)
        value_sum = sums[1] + jnp.einsum('bnh,bnhd->nhd', chances_low, far_grads)
        return ((key_sum, value_sum), None)
    initial = jnp.zeros((NLON, H, D // H), jnp.float32)
    sums, unused = lax.scan(add_line, (initial, initial), offsets_list())
    return ((sums[0] * factor).reshape(NLON, D), sums[1].reshape(NLON, D))

def reference(tokens, norm_gain, w_qkv, w_out, cotangent):
    source = tokens.astype(jnp.float32)
    inverse = lax.rsqrt(lax.optimization_barrier(jnp.mean(source * source, axis=-1, keepdims=True)) + epsilon)
    normed = (source * inverse * norm_gain).astype(jnp.bfloat16)
    flat_normed = normed.reshape(-1, D)
    packed = jnp.dot(flat_normed, w_qkv, preferred_element_type=jnp.float32).astype(jnp.bfloat16)
    packed = packed.reshape(NLAT, NLON, 3 * D)
    queries = packed[..., :D]
    keys = packed[..., D:2 * D]
    values = packed[..., 2 * D:]
    keys_ext = extend(keys)
    values_ext = extend(values)
    row_indices = jnp.arange(NLAT).astype(jnp.int32)

    def forward_map(row_index):
        return forward_row(row_index, queries, keys_ext, values_ext)
    attended, totals = lax.map(forward_map, row_indices)
    attended_flat = attended.reshape(-1, D)
    grad_flat = cotangent.reshape(-1, D)
    source_flat = source.reshape(-1, D)
    mixed = jnp.dot(attended_flat, w_out, preferred_element_type=jnp.float32) + source_flat
    result = mixed.astype(jnp.bfloat16).reshape(NLAT, NLON, D)
    factor_grad = (NLAT * NLON) ** (-0.5)
    grad_w_out = jnp.dot(attended_flat.T, grad_flat, preferred_element_type=jnp.float32) * factor_grad
    grad_attended = jnp.dot(grad_flat, w_out.T, preferred_element_type=jnp.float32).astype(jnp.bfloat16)
    product = grad_attended.astype(jnp.float32) * attended_flat.astype(jnp.float32)
    deltas = product.reshape(NLAT, NLON, H, D // H).sum(axis=-1)
    grad_grid = grad_attended.reshape(NLAT, NLON, D)

    def query_map(row_index):
        return query_row(row_index, queries, grad_grid, totals, deltas, keys_ext, values_ext)
    grad_query = lax.map(query_map, row_indices)
    queries_ext = extend(queries)
    grads_ext = extend(grad_grid)
    totals_ext = extend(totals)
    deltas_ext = extend(deltas)

    def key_map(row_index):
        return key_row(row_index, keys, values, queries_ext, grads_ext, totals_ext, deltas_ext)
    grad_key, grad_value = lax.map(key_map, row_indices)
    grad_packed = jnp.concatenate([grad_query, grad_key, grad_value], axis=-1).astype(jnp.bfloat16).reshape(-1, 3 * D)
    grad_w_qkv = jnp.dot(flat_normed.T, grad_packed, preferred_element_type=jnp.float32) * factor_grad
    grad_normed = jnp.dot(grad_packed, w_qkv.T, preferred_element_type=jnp.float32)
    scaled = norm_gain * grad_normed
    inverse_flat = inverse.reshape(-1, 1)
    grad_tokens = grad_flat.astype(jnp.float32) + inverse_flat * scaled - source_flat * inverse_flat ** 3 * lax.optimization_barrier(jnp.mean(source_flat * scaled, axis=-1, keepdims=True))
    return (result, grad_tokens.astype(jnp.bfloat16).reshape(NLAT, NLON, D), grad_w_qkv, grad_w_out)
```

```python
import jax
import jax.numpy as jnp
from jax import lax
from jax.experimental import pallas as pl
from jax.experimental.pallas import tpu as pltpu
from jax.sharding import PartitionSpec as P

H = 16
R = 6
SIDE_COLS = 8
PAIR = 128
TILE_ROWS = 8

epsilon = 1e-06
floor_score = -1e30

NT = (((1,), (1,)), ((), ()))


def dot(a, b, dims=(((1,), (0,)), ((), ()))):
    return lax.dot_general(a, b, dims, preferred_element_type=jnp.float32)


def attention_kernel(cols, row_count, q_ref, k_ref, v_ref, do_ref, o_ref, dq_ref, dk_ref, dv_ref, mask_ref):
    width = cols + 2 * SIDE_COLS
    queries = TILE_ROWS * cols
    keys = (TILE_ROWS + 2 * R) * width
    step = TILE_ROWS * width
    head = PAIR // 2

    @pl.when(pl.program_id(0) == 0)
    def _():
        key = lax.broadcasted_iota(jnp.int32, (keys, 2 * queries), 0)
        query = lax.rem(lax.broadcasted_iota(jnp.int32, (keys, 2 * queries), 1), queries)
        row_gap = lax.div(key, width) - lax.div(query, cols)
        place = lax.rem(key, width)
        place = jnp.where(
            place < cols,
            place,
            jnp.where(place < cols + SIDE_COLS, place - cols - SIDE_COLS, place - SIDE_COLS),
        )
        col_gap = place - lax.rem(query, cols)
        allowed = (row_gap >= 0) & (row_gap <= 2 * R) & (col_gap >= -R) & (col_gap <= R)
        mask_ref[...] = jnp.where(allowed, 0.0, floor_score)

    upper = lax.broadcasted_iota(jnp.int32, (2 * queries, PAIR), 0) < queries
    left = lax.broadcasted_iota(jnp.int32, (2 * queries, PAIR), 1) < head
    own = upper == left
    upper_t = lax.broadcasted_iota(jnp.int32, (PAIR, 2 * queries), 0) < head
    left_t = lax.broadcasted_iota(jnp.int32, (PAIR, 2 * queries), 1) < queries
    own_t = upper_t == left_t

    def paired(rows):
        twice = jnp.concatenate([rows, rows], axis=0)
        return jnp.where(own, twice, 0.0)

    def unpaired(both):
        picked = jnp.where(own_t, both, 0.0)
        return jnp.transpose(picked[:, :queries] + picked[:, queries:])

    k_all_t = jnp.transpose(k_ref[...])
    v_all_t = jnp.transpose(v_ref[...])
    dks, dvs = [], []
    for tile in range(row_count // TILE_ROWS):
        own_rows = slice(tile * queries, (tile + 1) * queries)
        own_keys = slice(tile * step, tile * step + keys)
        k = k_ref[own_keys, :]
        v = v_ref[own_keys, :]
        k_t = k_all_t[:, own_keys]
        v_t = v_all_t[:, own_keys]
        q32 = q_ref[own_rows, :].astype(jnp.float32) * (head ** (-0.5))
        do32 = do_ref[own_rows, :].astype(jnp.float32)
        q_pair = paired(q32).astype(jnp.bfloat16)
        do_pair32 = paired(do32)
        do_pair = do_pair32.astype(jnp.bfloat16)
        scores = dot(k, q_pair, NT) + mask_ref[...]
        highest = jnp.max(scores, axis=0, keepdims=True)
        raised = jnp.exp(scores - highest)
        chances = raised * (1.0 / jnp.sum(raised, axis=0, keepdims=True))
        chances_low = chances.astype(jnp.bfloat16)
        attended_t = dot(v_t, chances_low).astype(jnp.bfloat16).astype(jnp.float32)
        delta = jnp.sum(attended_t * jnp.transpose(do_pair32), axis=0, keepdims=True)
        o_ref[own_rows, :] = unpaired(attended_t).astype(jnp.bfloat16)
        grad_chances = dot(v, do_pair, NT)
        grad_scores = (chances * (grad_chances - delta)).astype(jnp.bfloat16)
        dq_ref[own_rows, :] = (unpaired(dot(k_t, grad_scores)) * (head ** (-0.5))).astype(
            jnp.bfloat16
        )
        dks.append(dot(grad_scores, q_pair))
        dvs.append(dot(chances_low, do_pair))

    for ref, parts in ((dk_ref, dks), (dv_ref, dvs)):
        for block in range(row_count // TILE_ROWS + (2 * R + TILE_ROWS - 1) // TILE_ROWS):
            low = block * step
            high = min(low + step, ref.shape[0])
            summed = None
            for tile, part in enumerate(parts):
                start = low - tile * step
                stop = min(high - tile * step, keys)
                if start < 0 or start >= keys:
                    continue
                piece = part[start:stop]
                if stop - start < high - low:
                    piece = jnp.concatenate(
                        [piece, jnp.zeros((high - low - stop + start, PAIR), jnp.float32)], axis=0
                    )
                summed = piece if summed is None else summed + piece
            ref[low:high, :] = summed.astype(jnp.bfloat16)


def attention(query, keyval, grad_attended, row_count, cols):
    cells, width_model = query.shape
    frame_cells = keyval.shape[0]
    pairs = width_model // PAIR
    keys = (TILE_ROWS + 2 * R) * (cols + 2 * SIDE_COLS)
    one = lambda rows, shift=0: pl.BlockSpec((rows, PAIR), lambda i: (0, i + shift))
    low = lambda rows: jax.ShapeDtypeStruct((rows, width_model), jnp.bfloat16)

    def kernel(*refs):
        attention_kernel(cols, row_count, *refs)

    return pl.pallas_call(
        kernel,
        grid=(pairs,),
        in_specs=[one(cells), one(frame_cells), one(frame_cells, pairs), one(cells)],
        out_specs=[one(cells), one(cells), one(frame_cells), one(frame_cells)],
        out_shape=[low(cells), low(cells), low(frame_cells), low(frame_cells)],
        scratch_shapes=[pltpu.VMEM((keys, 2 * TILE_ROWS * cols), jnp.float32)],
        compiler_params=pltpu.CompilerParams(vmem_limit_bytes=40 << 20),
        cost_estimate=pl.CostEstimate(
            flops=24 * cells * keys * width_model, bytes_accessed=16 << 20, transcendentals=cells * keys * H
        ),
    )(query, keyval, keyval, grad_attended)


def to_next(value, axis):
    count = lax.axis_size(axis)
    return lax.ppermute(value, axis, [(i, (i + 1) % count) for i in range(count)])


def to_previous(value, axis):
    count = lax.axis_size(axis)
    return lax.ppermute(value, axis, [((i + 1) % count, i) for i in range(count)])


def south_to_north(value):
    count = lax.axis_size("lat")
    return lax.ppermute(value, "lat", [(i + 1, i) for i in range(count - 1)])


def north_to_south(value):
    count = lax.axis_size("lat")
    return lax.ppermute(value, "lat", [(i, i + 1) for i in range(count - 1)])


def across_pole(value):
    lats = lax.axis_size("lat")
    lons = lax.axis_size("lon")
    pairs = [
        (lat * lons + lon, lat * lons + (lon + lons // 2) % lons)
        for lat in (0, lats - 1)
        for lon in range(lons)
    ]
    return lax.ppermute(value, ("lat", "lon"), pairs)


def shards(tokens, norm_gain, w_qkv, w_out, cotangent):
    rows, cols, width = tokens.shape
    lat_count = lax.axis_size("lat")
    device_count = lat_count * lax.axis_size("lon")
    at_north = lax.axis_index("lat") == 0
    at_south = lax.axis_index("lat") == lat_count - 1
    grad_scale = (rows * cols * device_count) ** (-0.5)
    side = SIDE_COLS

    west_mid = to_next(tokens[:, cols - side :], "lon")
    east_mid = to_previous(tokens[:, :side], "lon")
    top, bottom = tokens[:R], tokens[rows - R :]
    from_north = north_to_south(bottom)
    from_south = south_to_north(top)
    mirrored = across_pole(jnp.where(at_north, top, bottom)[::-1])
    top_in = jnp.where(at_north, mirrored, from_north)
    bottom_in = jnp.where(at_south, mirrored, from_south)
    edge = jnp.concatenate([top_in, bottom_in], axis=0)
    west_edge = to_next(edge[:, cols - side :], "lon")
    east_edge = to_previous(edge[:, :side], "lon")
    frame = jnp.concatenate(
        [
            jnp.concatenate([top_in, west_edge[:R], east_edge[:R]], axis=1),
            jnp.concatenate([tokens, west_mid, east_mid], axis=1),
            jnp.concatenate([bottom_in, west_edge[R:], east_edge[R:]], axis=1),
        ],
        axis=0,
    )
    frame_rows, frame_cols = frame.shape[:2]

    def normalise(cells):
        source = cells.astype(jnp.float32)
        inverse = lax.rsqrt(jnp.mean(source * source, axis=-1, keepdims=True) + epsilon)
        return (source * inverse * norm_gain).astype(jnp.bfloat16), source, inverse

    normed, source, inverse = normalise(tokens.reshape(-1, width))
    normed_frame = normalise(frame.reshape(-1, width))[0]
    w_query, w_keyval = w_qkv[:, :width], w_qkv[:, width:]
    query = dot(normed, w_query).astype(jnp.bfloat16)
    grad_flat = cotangent.reshape(-1, width)
    grad_attended = dot(grad_flat, w_out, NT).astype(jnp.bfloat16)
    keyval = dot(normed_frame, w_keyval).astype(jnp.bfloat16)
    attended, grad_query, grad_key, grad_value = attention(query, keyval, grad_attended, rows, cols)

    TN = (((0,), (0,)), ((), ()))
    qkv_term = jnp.concatenate(
        [
            dot(normed, grad_query, TN).astype(jnp.bfloat16),
            dot(normed_frame, grad_key, TN).astype(jnp.bfloat16),
            dot(normed_frame, grad_value, TN).astype(jnp.bfloat16),
        ],
        axis=1,
    )
    out_term = dot(attended, grad_flat, TN).astype(jnp.bfloat16)
    qkv_share = lax.psum_scatter(qkv_term, ("lat", "lon"), scatter_dimension=0, tiled=True)
    out_share = lax.psum_scatter(out_term, ("lat", "lon"), scatter_dimension=0, tiled=True)

    result = (dot(attended, w_out) + source).astype(jnp.bfloat16).reshape(rows, cols, width)

    spread = dot(grad_key, w_keyval[:, :width], NT) + dot(grad_value, w_keyval[:, width:], NT)
    spread = spread.reshape(frame_rows, frame_cols, width)
    strips = spread[:, cols:].astype(jnp.bfloat16)
    edges = jnp.concatenate([strips[:R], strips[R + rows :]], axis=0)
    west_edge_back = to_previous(edges[:, :side], "lon").astype(jnp.float32)
    east_edge_back = to_next(edges[:, side:], "lon").astype(jnp.float32)
    west_back = to_previous(strips[R : R + rows, :side], "lon").astype(jnp.float32)
    east_back = to_next(strips[R : R + rows, side:], "lon").astype(jnp.float32)
    edge_sum = jnp.concatenate([spread[:R, :cols], spread[R + rows :, :cols]], axis=0)
    edge_sum = edge_sum + jnp.concatenate([east_edge_back, west_edge_back], axis=1)
    edge_low = edge_sum.astype(jnp.bfloat16)
    top_out, bottom_out = edge_low[:R], edge_low[R:]
    to_north = south_to_north(top_out).astype(jnp.float32)
    to_south = north_to_south(bottom_out).astype(jnp.float32)
    pole_back = across_pole(jnp.where(at_north, top_out, bottom_out)[::-1]).astype(jnp.float32)
    top_back = jnp.where(at_north, pole_back, to_south)
    bottom_back = jnp.where(at_south, pole_back, to_north)
    grad_normed = spread[R : R + rows, :cols] + jnp.concatenate([east_back, west_back], axis=1)
    grad_normed = grad_normed + dot(grad_query, w_query, NT).reshape(rows, cols, width)
    gap = jnp.zeros((rows - R, cols, width), jnp.float32)
    grad_normed = grad_normed + jnp.concatenate([top_back, gap], axis=0)
    grad_normed = grad_normed + jnp.concatenate([gap, bottom_back], axis=0)

    scaled = norm_gain * grad_normed.reshape(-1, width)
    grad_input = (
        grad_flat.astype(jnp.float32)
        + inverse * scaled
        - source * inverse**3 * jnp.mean(source * scaled, axis=-1, keepdims=True)
    )
    grad_tokens = grad_input.astype(jnp.bfloat16).reshape(rows, cols, width)
    return (
        result,
        grad_tokens,
        qkv_share.astype(jnp.float32) * grad_scale,
        out_share.astype(jnp.float32) * grad_scale,
    )


def solution(mesh):
    placed = (P("lat", "lon", None), P(), P(), P(), P("lat", "lon", None))
    return jax.shard_map(
        shards,
        mesh=mesh,
        in_specs=placed,
        out_specs=(
            P("lat", "lon", None),
            P("lat", "lon", None),
            P(("lat", "lon"), None),
            P(("lat", "lon"), None),
        ),
        check_vma=False,
    )
```

```python
import jax
import jax.numpy as jnp
from jax import lax
from jax.experimental import pallas as pl
from jax.experimental.pallas import tpu as pltpu
from jax.sharding import PartitionSpec as P

H = 16
R = 6
SIDE_COLS = 8
PAIR = 128
TILE_ROWS = 8

epsilon = 1e-06
floor_score = -1e30

NT = (((1,), (1,)), ((), ()))


def dot(a, b, dims=(((1,), (0,)), ((), ()))):
    return lax.dot_general(a, b, dims, preferred_element_type=jnp.float32)


def attention_kernel(cols, row_count, q_ref, k_ref, v_ref, do_ref, o_ref, dq_ref, dk_ref, dv_ref, mask_ref):
    width = cols + 2 * SIDE_COLS
    queries = TILE_ROWS * cols
    keys = (TILE_ROWS + 2 * R) * width
    step = TILE_ROWS * width
    head = PAIR // 2

    @pl.when(pl.program_id(0) == 0)
    def _():
        key = lax.broadcasted_iota(jnp.int32, (keys, 2 * queries), 0)
        query = lax.rem(lax.broadcasted_iota(jnp.int32, (keys, 2 * queries), 1), queries)
        row_gap = lax.div(key, width) - lax.div(query, cols)
        place = lax.rem(key, width)
        place = jnp.where(
            place < cols,
            place,
            jnp.where(place < cols + SIDE_COLS, place - cols - SIDE_COLS, place - SIDE_COLS),
        )
        col_gap = place - lax.rem(query, cols)
        allowed = (row_gap >= 0) & (row_gap <= 2 * R) & (col_gap >= -R) & (col_gap <= R)
        mask_ref[...] = jnp.where(allowed, 0.0, floor_score)

    upper = lax.broadcasted_iota(jnp.int32, (2 * queries, PAIR), 0) < queries
    left = lax.broadcasted_iota(jnp.int32, (2 * queries, PAIR), 1) < head
    own = upper == left
    upper_t = lax.broadcasted_iota(jnp.int32, (PAIR, 2 * queries), 0) < head
    left_t = lax.broadcasted_iota(jnp.int32, (PAIR, 2 * queries), 1) < queries
    own_t = upper_t == left_t

    def paired(rows):
        twice = jnp.concatenate([rows, rows], axis=0)
        return jnp.where(own, twice, 0.0)

    def unpaired(both):
        picked = jnp.where(own_t, both, 0.0)
        return jnp.transpose(picked[:, :queries] + picked[:, queries:])

    k_all_t = jnp.transpose(k_ref[...])
    v_all_t = jnp.transpose(v_ref[...])
    dks, dvs = [], []
    for tile in range(row_count // TILE_ROWS):
        own_rows = slice(tile * queries, (tile + 1) * queries)
        own_keys = slice(tile * step, tile * step + keys)
        k = k_ref[own_keys, :]
        v = v_ref[own_keys, :]
        k_t = k_all_t[:, own_keys]
        v_t = v_all_t[:, own_keys]
        q32 = q_ref[own_rows, :].astype(jnp.float32) * (head ** (-0.5))
        do32 = do_ref[own_rows, :].astype(jnp.float32)
        q_pair = paired(q32).astype(jnp.bfloat16)
        do_pair32 = paired(do32)
        do_pair = do_pair32.astype(jnp.bfloat16)
        scores = dot(k, q_pair, NT) + mask_ref[...]
        highest = jnp.max(scores, axis=0, keepdims=True)
        raised = jnp.exp(scores - highest)
        chances = raised * (1.0 / jnp.sum(raised, axis=0, keepdims=True))
        chances_low = chances.astype(jnp.bfloat16)
        attended_t = dot(v_t, chances_low).astype(jnp.bfloat16).astype(jnp.float32)
        delta = jnp.sum(attended_t * jnp.transpose(do_pair32), axis=0, keepdims=True)
        o_ref[own_rows, :] = unpaired(attended_t).astype(jnp.bfloat16)
        grad_chances = dot(v, do_pair, NT)
        grad_scores = (chances * (grad_chances - delta)).astype(jnp.bfloat16)
        dq_ref[own_rows, :] = (unpaired(dot(k_t, grad_scores)) * (head ** (-0.5))).astype(
            jnp.bfloat16
        )
        dks.append(dot(grad_scores, q_pair))
        dvs.append(dot(chances_low, do_pair))

    for ref, parts in ((dk_ref, dks), (dv_ref, dvs)):
        for block in range(row_count // TILE_ROWS + (2 * R + TILE_ROWS - 1) // TILE_ROWS):
            low = block * step
            high = min(low + step, ref.shape[0])
            summed = None
            for tile, part in enumerate(parts):
                start = low - tile * step
                stop = min(high - tile * step, keys)
                if start < 0 or start >= keys:
                    continue
                piece = part[start:stop]
                if stop - start < high - low:
                    piece = jnp.concatenate(
                        [piece, jnp.zeros((high - low - stop + start, PAIR), jnp.float32)], axis=0
                    )
                summed = piece if summed is None else summed + piece
            ref[low:high, :] = summed.astype(jnp.bfloat16)


def attention(query, keyval, grad_attended, row_count, cols):
    cells, width_model = query.shape
    frame_cells = keyval.shape[0]
    pairs = width_model // PAIR
    keys = (TILE_ROWS + 2 * R) * (cols + 2 * SIDE_COLS)
    one = lambda rows, shift=0: pl.BlockSpec((rows, PAIR), lambda i: (0, i + shift))
    low = lambda rows: jax.ShapeDtypeStruct((rows, width_model), jnp.bfloat16)

    def kernel(*refs):
        attention_kernel(cols, row_count, *refs)

    return pl.pallas_call(
        kernel,
        grid=(pairs,),
        in_specs=[one(cells), one(frame_cells), one(frame_cells, pairs), one(cells)],
        out_specs=[one(cells), one(cells), one(frame_cells), one(frame_cells)],
        out_shape=[low(cells), low(cells), low(frame_cells), low(frame_cells)],
        scratch_shapes=[pltpu.VMEM((keys, 2 * TILE_ROWS * cols), jnp.float32)],
        compiler_params=pltpu.CompilerParams(vmem_limit_bytes=40 << 20),
        cost_estimate=pl.CostEstimate(
            flops=24 * cells * keys * width_model, bytes_accessed=16 << 20, transcendentals=cells * keys * H
        ),
    )(query, keyval, keyval, grad_attended)


def to_next(value, axis):
    count = lax.axis_size(axis)
    return lax.ppermute(value, axis, [(i, (i + 1) % count) for i in range(count)])


def to_previous(value, axis):
    count = lax.axis_size(axis)
    return lax.ppermute(value, axis, [((i + 1) % count, i) for i in range(count)])


def south_to_north(value):
    count = lax.axis_size("lat")
    return lax.ppermute(value, "lat", [(i + 1, i) for i in range(count - 1)])


def north_to_south(value):
    count = lax.axis_size("lat")
    return lax.ppermute(value, "lat", [(i, i + 1) for i in range(count - 1)])


def across_pole(value):
    lats = lax.axis_size("lat")
    lons = lax.axis_size("lon")
    pairs = [
        (lat * lons + lon, lat * lons + (lon + lons // 2) % lons)
        for lat in (0, lats - 1)
        for lon in range(lons)
    ]
    return lax.ppermute(value, ("lat", "lon"), pairs)


def halved(term, places, order):
    places = list(places)
    for axis, bit in order:
        at = places.index((axis, bit))
        places.pop(at)
        outer, inner = 2**at, term.shape[0] // 2 ** (at + 1)
        blocks = term.reshape(outer, 2, inner, term.shape[1])
        upper = (lax.axis_index(axis) // 2**bit) % 2 == 1
        first, second = blocks[:, 0], blocks[:, 1]
        sent = jnp.where(upper, first, second)
        kept = jnp.where(upper, second, first)
        pairs = [(i, i ^ (1 << bit)) for i in range(lax.axis_size(axis))]
        came = lax.ppermute(sent, axis, pairs)
        total = kept.astype(jnp.float32) + came.astype(jnp.float32)
        total = total.reshape(outer * inner, term.shape[1])
        term = total if not places else total.astype(jnp.bfloat16)
    return term, places


def shards(tokens, norm_gain, w_qkv, w_out, cotangent):
    rows, cols, width = tokens.shape
    lat_count = lax.axis_size("lat")
    device_count = lat_count * lax.axis_size("lon")
    at_north = lax.axis_index("lat") == 0
    at_south = lax.axis_index("lat") == lat_count - 1
    grad_scale = (rows * cols * device_count) ** (-0.5)
    side = SIDE_COLS

    west_mid = to_next(tokens[:, cols - side :], "lon")
    east_mid = to_previous(tokens[:, :side], "lon")
    top, bottom = tokens[:R], tokens[rows - R :]
    from_north = north_to_south(bottom)
    from_south = south_to_north(top)
    mirrored = across_pole(jnp.where(at_north, top, bottom)[::-1])
    top_in = jnp.where(at_north, mirrored, from_north)
    bottom_in = jnp.where(at_south, mirrored, from_south)
    edge = jnp.concatenate([top_in, bottom_in], axis=0)
    west_edge = to_next(edge[:, cols - side :], "lon")
    east_edge = to_previous(edge[:, :side], "lon")
    frame = jnp.concatenate(
        [
            jnp.concatenate([top_in, west_edge[:R], east_edge[:R]], axis=1),
            jnp.concatenate([tokens, west_mid, east_mid], axis=1),
            jnp.concatenate([bottom_in, west_edge[R:], east_edge[R:]], axis=1),
        ],
        axis=0,
    )
    frame_rows, frame_cols = frame.shape[:2]

    def normalise(cells):
        source = cells.astype(jnp.float32)
        inverse = lax.rsqrt(jnp.mean(source * source, axis=-1, keepdims=True) + epsilon)
        return (source * inverse * norm_gain).astype(jnp.bfloat16), source, inverse

    normed, source, inverse = normalise(tokens.reshape(-1, width))
    normed_frame = normalise(frame.reshape(-1, width))[0]
    w_query, w_keyval = w_qkv[:, :width], w_qkv[:, width:]
    query = dot(normed, w_query).astype(jnp.bfloat16)
    grad_flat = cotangent.reshape(-1, width)
    grad_attended = dot(grad_flat, w_out, NT).astype(jnp.bfloat16)
    keyval = dot(normed_frame, w_keyval).astype(jnp.bfloat16)
    attended, grad_query, grad_key, grad_value = attention(query, keyval, grad_attended, rows, cols)

    TN = (((0,), (0,)), ((), ()))
    lat_bits = range(lat_count.bit_length() - 1)
    lon_bits = range(lax.axis_size("lon").bit_length() - 1)
    low_first = [("lat", bit) for bit in lat_bits] + [("lon", 0)]
    low_first += [("lon", bit) for bit in reversed(lon_bits) if bit > 0]
    lon_first = [("lat", 0), ("lon", 0), ("lon", len(lon_bits) - 1)]
    lon_first += [("lat", bit) for bit in lat_bits if bit > 0]
    lon_first += [("lon", bit) for bit in reversed(lon_bits) if 0 < bit < len(lon_bits) - 1]
    places = [("lat", bit) for bit in reversed(lat_bits)]
    places += [("lon", bit) for bit in reversed(lon_bits)]
    split = len(lat_bits)
    out_term = dot(attended, grad_flat, TN).astype(jnp.bfloat16)
    out_part, left_over = halved(out_term, places, low_first[:split])
    query_term = dot(normed, grad_query, TN).astype(jnp.bfloat16)
    query_part, left_over = halved(query_term, places, low_first[:split])
    keyval_term = dot(normed_frame, jnp.concatenate([grad_key, grad_value], axis=1), TN)
    keyval_share, none = halved(keyval_term.astype(jnp.bfloat16), places, lon_first)
    pair_part = jnp.concatenate([query_part, out_part], axis=1)
    pair_share, none = halved(pair_part, left_over, low_first[split:])
    qkv_share = jnp.concatenate([pair_share[:, :width], keyval_share], axis=1)
    out_share = pair_share[:, width:]

    result = (dot(attended, w_out) + source).astype(jnp.bfloat16).reshape(rows, cols, width)

    spread = dot(grad_key, w_keyval[:, :width], NT) + dot(grad_value, w_keyval[:, width:], NT)
    spread = spread.reshape(frame_rows, frame_cols, width)
    strips = spread[:, cols:].astype(jnp.bfloat16)
    edges = jnp.concatenate([strips[:R], strips[R + rows :]], axis=0)
    west_edge_back = to_previous(edges[:, :side], "lon").astype(jnp.float32)
    east_edge_back = to_next(edges[:, side:], "lon").astype(jnp.float32)
    west_back = to_previous(strips[R : R + rows, :side], "lon").astype(jnp.float32)
    east_back = to_next(strips[R : R + rows, side:], "lon").astype(jnp.float32)
    edge_sum = jnp.concatenate([spread[:R, :cols], spread[R + rows :, :cols]], axis=0)
    edge_sum = edge_sum + jnp.concatenate([east_edge_back, west_edge_back], axis=1)
    edge_low = edge_sum.astype(jnp.bfloat16)
    top_out, bottom_out = edge_low[:R], edge_low[R:]
    to_north = south_to_north(top_out).astype(jnp.float32)
    to_south = north_to_south(bottom_out).astype(jnp.float32)
    pole_back = across_pole(jnp.where(at_north, top_out, bottom_out)[::-1]).astype(jnp.float32)
    top_back = jnp.where(at_north, pole_back, to_south)
    bottom_back = jnp.where(at_south, pole_back, to_north)
    grad_normed = spread[R : R + rows, :cols] + jnp.concatenate([east_back, west_back], axis=1)
    grad_normed = grad_normed + dot(grad_query, w_query, NT).reshape(rows, cols, width)
    gap = jnp.zeros((rows - R, cols, width), jnp.float32)
    grad_normed = grad_normed + jnp.concatenate([top_back, gap], axis=0)
    grad_normed = grad_normed + jnp.concatenate([gap, bottom_back], axis=0)

    scaled = norm_gain * grad_normed.reshape(-1, width)
    grad_input = (
        grad_flat.astype(jnp.float32)
        + inverse * scaled
        - source * inverse**3 * jnp.mean(source * scaled, axis=-1, keepdims=True)
    )
    grad_tokens = grad_input.astype(jnp.bfloat16).reshape(rows, cols, width)
    return (
        result,
        grad_tokens,
        qkv_share.astype(jnp.float32) * grad_scale,
        out_share.astype(jnp.float32) * grad_scale,
    )


def solution(mesh):
    placed = (P("lat", "lon", None), P(), P(), P(), P("lat", "lon", None))
    return jax.shard_map(
        shards,
        mesh=mesh,
        in_specs=placed,
        out_specs=(
            P("lat", "lon", None),
            P("lat", "lon", None),
            P(("lat", "lon"), None),
            P(("lat", "lon"), None),
        ),
        check_vma=False,
    )
```

```python
import jax
import jax.numpy as jnp
from jax import lax
from jax.experimental import pallas as pl
from jax.experimental.pallas import tpu as pltpu
from jax.sharding import PartitionSpec as P

H = 16
R = 6
SIDE_COLS = 8
PAIR = 128
TILE_ROWS = 8

epsilon = 1e-06
floor_score = -1e30

NT = (((1,), (1,)), ((), ()))


def dot(a, b, dims=(((1,), (0,)), ((), ()))):
    return lax.dot_general(a, b, dims, preferred_element_type=jnp.float32)


def attention_kernel(cols, row_count, q_ref, k_ref, v_ref, do_ref, o_ref, dq_ref, dk_ref, dv_ref, mask_ref):
    width = cols + 2 * SIDE_COLS
    queries = TILE_ROWS * cols
    keys = (TILE_ROWS + 2 * R) * width
    step = TILE_ROWS * width
    head = PAIR // 2

    @pl.when(pl.program_id(0) == 0)
    def _():
        key = lax.broadcasted_iota(jnp.int32, (keys, 2 * queries), 0)
        query = lax.rem(lax.broadcasted_iota(jnp.int32, (keys, 2 * queries), 1), queries)
        row_gap = lax.div(key, width) - lax.div(query, cols)
        place = lax.rem(key, width)
        place = jnp.where(
            place < cols,
            place,
            jnp.where(place < cols + SIDE_COLS, place - cols - SIDE_COLS, place - SIDE_COLS),
        )
        col_gap = place - lax.rem(query, cols)
        allowed = (row_gap >= 0) & (row_gap <= 2 * R) & (col_gap >= -R) & (col_gap <= R)
        mask_ref[...] = jnp.where(allowed, 0.0, floor_score)

    upper = lax.broadcasted_iota(jnp.int32, (2 * queries, PAIR), 0) < queries
    left = lax.broadcasted_iota(jnp.int32, (2 * queries, PAIR), 1) < head
    own = upper == left
    upper_t = lax.broadcasted_iota(jnp.int32, (PAIR, 2 * queries), 0) < head
    left_t = lax.broadcasted_iota(jnp.int32, (PAIR, 2 * queries), 1) < queries
    own_t = upper_t == left_t

    def paired(rows):
        twice = jnp.concatenate([rows, rows], axis=0)
        return jnp.where(own, twice, 0.0)

    def unpaired(both):
        picked = jnp.where(own_t, both, 0.0)
        return jnp.transpose(picked[:, :queries] + picked[:, queries:])

    k_all_t = jnp.transpose(k_ref[...])
    v_all_t = jnp.transpose(v_ref[...])
    dks, dvs = [], []
    for tile in range(row_count // TILE_ROWS):
        own_rows = slice(tile * queries, (tile + 1) * queries)
        own_keys = slice(tile * step, tile * step + keys)
        k = k_ref[own_keys, :]
        v = v_ref[own_keys, :]
        k_t = k_all_t[:, own_keys]
        v_t = v_all_t[:, own_keys]
        q32 = q_ref[own_rows, :].astype(jnp.float32) * (head ** (-0.5))
        do32 = do_ref[own_rows, :].astype(jnp.float32)
        q_pair = paired(q32).astype(jnp.bfloat16)
        do_pair32 = paired(do32)
        do_pair = do_pair32.astype(jnp.bfloat16)
        scores = dot(k, q_pair, NT) + mask_ref[...]
        highest = jnp.max(scores, axis=0, keepdims=True)
        raised = jnp.exp(scores - highest)
        chances = raised * (1.0 / jnp.sum(raised, axis=0, keepdims=True))
        chances_low = chances.astype(jnp.bfloat16)
        attended_t = dot(v_t, chances_low).astype(jnp.bfloat16).astype(jnp.float32)
        delta = jnp.sum(attended_t * jnp.transpose(do_pair32), axis=0, keepdims=True)
        o_ref[own_rows, :] = unpaired(attended_t).astype(jnp.bfloat16)
        grad_chances = dot(v, do_pair, NT)
        grad_scores = (chances * (grad_chances - delta)).astype(jnp.bfloat16)
        dq_ref[own_rows, :] = (unpaired(dot(k_t, grad_scores)) * (head ** (-0.5))).astype(
            jnp.bfloat16
        )
        dks.append(dot(grad_scores, q_pair))
        dvs.append(dot(chances_low, do_pair))

    for ref, parts in ((dk_ref, dks), (dv_ref, dvs)):
        for block in range(row_count // TILE_ROWS + (2 * R + TILE_ROWS - 1) // TILE_ROWS):
            low = block * step
            high = min(low + step, ref.shape[0])
            summed = None
            for tile, part in enumerate(parts):
                start = low - tile * step
                stop = min(high - tile * step, keys)
                if start < 0 or start >= keys:
                    continue
                piece = part[start:stop]
                if stop - start < high - low:
                    piece = jnp.concatenate(
                        [piece, jnp.zeros((high - low - stop + start, PAIR), jnp.float32)], axis=0
                    )
                summed = piece if summed is None else summed + piece
            ref[low:high, :] = summed.astype(jnp.bfloat16)


def attention(query, keyval, grad_attended, row_count, cols):
    cells, width_model = query.shape
    frame_cells = keyval.shape[0]
    pairs = width_model // PAIR
    keys = (TILE_ROWS + 2 * R) * (cols + 2 * SIDE_COLS)
    one = lambda rows, shift=0: pl.BlockSpec((rows, PAIR), lambda i: (0, i + shift))
    low = lambda rows: jax.ShapeDtypeStruct((rows, width_model), jnp.bfloat16)

    def kernel(*refs):
        attention_kernel(cols, row_count, *refs)

    return pl.pallas_call(
        kernel,
        grid=(pairs,),
        in_specs=[one(cells), one(frame_cells), one(frame_cells, pairs), one(cells)],
        out_specs=[one(cells), one(cells), one(frame_cells), one(frame_cells)],
        out_shape=[low(cells), low(cells), low(frame_cells), low(frame_cells)],
        scratch_shapes=[pltpu.VMEM((keys, 2 * TILE_ROWS * cols), jnp.float32)],
        compiler_params=pltpu.CompilerParams(vmem_limit_bytes=40 << 20),
        cost_estimate=pl.CostEstimate(
            flops=24 * cells * keys * width_model, bytes_accessed=16 << 20, transcendentals=cells * keys * H
        ),
    )(query, keyval, keyval, grad_attended)


def to_next(value, axis):
    count = lax.axis_size(axis)
    return lax.ppermute(value, axis, [(i, (i + 1) % count) for i in range(count)])


def to_previous(value, axis):
    count = lax.axis_size(axis)
    return lax.ppermute(value, axis, [((i + 1) % count, i) for i in range(count)])


def south_to_north(value):
    count = lax.axis_size("lat")
    return lax.ppermute(value, "lat", [(i + 1, i) for i in range(count - 1)])


def north_to_south(value):
    count = lax.axis_size("lat")
    return lax.ppermute(value, "lat", [(i, i + 1) for i in range(count - 1)])


def across_pole(value):
    lats = lax.axis_size("lat")
    lons = lax.axis_size("lon")
    pairs = [
        (lat * lons + lon, lat * lons + (lon + lons // 2) % lons)
        for lat in (0, lats - 1)
        for lon in range(lons)
    ]
    return lax.ppermute(value, ("lat", "lon"), pairs)


def halved(term, places, order):
    places = list(places)
    for axis, bit in order:
        at = places.index((axis, bit))
        places.pop(at)
        outer, inner = 2**at, term.shape[0] // 2 ** (at + 1)
        blocks = term.reshape(outer, 2, inner, term.shape[1])
        upper = (lax.axis_index(axis) // 2**bit) % 2 == 1
        first, second = blocks[:, 0], blocks[:, 1]
        sent = jnp.where(upper, first, second)
        kept = jnp.where(upper, second, first)
        pairs = [(i, i ^ (1 << bit)) for i in range(lax.axis_size(axis))]
        came = lax.ppermute(sent, axis, pairs)
        total = kept.astype(jnp.float32) + came.astype(jnp.float32)
        total = total.reshape(outer * inner, term.shape[1])
        term = total if not places else total.astype(jnp.bfloat16)
    return term, places


def shards(tokens, norm_gain, w_qkv, w_out, cotangent):
    rows, cols, width = tokens.shape
    lat_count = lax.axis_size("lat")
    device_count = lat_count * lax.axis_size("lon")
    at_north = lax.axis_index("lat") == 0
    at_south = lax.axis_index("lat") == lat_count - 1
    grad_scale = (rows * cols * device_count) ** (-0.5)
    side = SIDE_COLS

    west_mid = to_next(tokens[:, cols - side :], "lon")
    east_mid = to_previous(tokens[:, :side], "lon")
    top, bottom = tokens[:R], tokens[rows - R :]
    from_north = north_to_south(bottom)
    from_south = south_to_north(top)
    mirrored = across_pole(jnp.where(at_north, top, bottom)[::-1])
    top_in = jnp.where(at_north, mirrored, from_north)
    bottom_in = jnp.where(at_south, mirrored, from_south)
    edge = jnp.concatenate([top_in, bottom_in], axis=0)
    west_edge = to_next(edge[:, cols - side :], "lon")
    east_edge = to_previous(edge[:, :side], "lon")
    frame = jnp.concatenate(
        [
            jnp.concatenate([top_in, west_edge[:R], east_edge[:R]], axis=1),
            jnp.concatenate([tokens, west_mid, east_mid], axis=1),
            jnp.concatenate([bottom_in, west_edge[R:], east_edge[R:]], axis=1),
        ],
        axis=0,
    )
    frame_rows, frame_cols = frame.shape[:2]

    def normalise(cells):
        source = cells.astype(jnp.float32)
        inverse = lax.rsqrt(jnp.mean(source * source, axis=-1, keepdims=True) + epsilon)
        return (source * inverse * norm_gain).astype(jnp.bfloat16), source, inverse

    normed, source, inverse = normalise(tokens.reshape(-1, width))
    normed_frame = normalise(frame.reshape(-1, width))[0]
    w_query, w_keyval = w_qkv[:, :width], w_qkv[:, width:]
    query = dot(normed, w_query).astype(jnp.bfloat16)
    grad_flat = cotangent.reshape(-1, width)
    grad_attended = dot(grad_flat, w_out, NT).astype(jnp.bfloat16)
    keyval = dot(normed_frame, w_keyval).astype(jnp.bfloat16)
    attended, grad_query, grad_key, grad_value = attention(query, keyval, grad_attended, rows, cols)

    TN = (((0,), (0,)), ((), ()))
    lat_bits = range(lat_count.bit_length() - 1)
    lon_bits = range(lax.axis_size("lon").bit_length() - 1)
    low_first = [("lat", bit) for bit in lat_bits] + [("lon", 0)]
    low_first += [("lon", bit) for bit in reversed(lon_bits) if bit > 0]
    lon_first = [("lat", 0), ("lon", 0), ("lon", len(lon_bits) - 1)]
    lon_first += [("lat", bit) for bit in lat_bits if bit > 0]
    lon_first += [("lon", bit) for bit in reversed(lon_bits) if 0 < bit < len(lon_bits) - 1]
    places = [("lat", bit) for bit in reversed(lat_bits)]
    places += [("lon", bit) for bit in reversed(lon_bits)]
    split = len(lat_bits)
    out_term = dot(attended, grad_flat, TN).astype(jnp.bfloat16)
    out_part, left_over = halved(out_term, places, low_first[:split])
    query_term = dot(normed, grad_query, TN).astype(jnp.bfloat16)
    query_part, left_over = halved(query_term, places, low_first[:split])
    keyval_term = dot(normed_frame, jnp.concatenate([grad_key, grad_value], axis=1), TN)
    keyval_part, left_keyval = halved(keyval_term.astype(jnp.bfloat16), places, lon_first[:1])
    keyval_part, grad_key, grad_value = lax.optimization_barrier(
        (keyval_part, grad_key, grad_value)
    )
    keyval_share, none = halved(keyval_part, left_keyval, lon_first[1:])
    pair_part = jnp.concatenate([query_part, out_part], axis=1)
    pair_share, none = halved(pair_part, left_over, low_first[split:])
    qkv_share = jnp.concatenate([pair_share[:, :width], keyval_share], axis=1)
    out_share = pair_share[:, width:]

    result = (dot(attended, w_out) + source).astype(jnp.bfloat16).reshape(rows, cols, width)

    spread = dot(grad_key, w_keyval[:, :width], NT) + dot(grad_value, w_keyval[:, width:], NT)
    spread = spread.reshape(frame_rows, frame_cols, width)
    strips = spread[:, cols:].astype(jnp.bfloat16)
    edges = jnp.concatenate([strips[:R], strips[R + rows :]], axis=0)
    west_edge_back = to_previous(edges[:, :side], "lon").astype(jnp.float32)
    east_edge_back = to_next(edges[:, side:], "lon").astype(jnp.float32)
    west_back = to_previous(strips[R : R + rows, :side], "lon").astype(jnp.float32)
    east_back = to_next(strips[R : R + rows, side:], "lon").astype(jnp.float32)
    edge_sum = jnp.concatenate([spread[:R, :cols], spread[R + rows :, :cols]], axis=0)
    edge_sum = edge_sum + jnp.concatenate([east_edge_back, west_edge_back], axis=1)
    edge_low = edge_sum.astype(jnp.bfloat16)
    top_out, bottom_out = edge_low[:R], edge_low[R:]
    to_north = south_to_north(top_out).astype(jnp.float32)
    to_south = north_to_south(bottom_out).astype(jnp.float32)
    pole_back = across_pole(jnp.where(at_north, top_out, bottom_out)[::-1]).astype(jnp.float32)
    top_back = jnp.where(at_north, pole_back, to_south)
    bottom_back = jnp.where(at_south, pole_back, to_north)
    grad_normed = spread[R : R + rows, :cols] + jnp.concatenate([east_back, west_back], axis=1)
    grad_normed = grad_normed + dot(grad_query, w_query, NT).reshape(rows, cols, width)
    gap = jnp.zeros((rows - R, cols, width), jnp.float32)
    grad_normed = grad_normed + jnp.concatenate([top_back, gap], axis=0)
    grad_normed = grad_normed + jnp.concatenate([gap, bottom_back], axis=0)

    scaled = norm_gain * grad_normed.reshape(-1, width)
    grad_input = (
        grad_flat.astype(jnp.float32)
        + inverse * scaled
        - source * inverse**3 * jnp.mean(source * scaled, axis=-1, keepdims=True)
    )
    grad_tokens = grad_input.astype(jnp.bfloat16).reshape(rows, cols, width)
    return (
        result,
        grad_tokens,
        qkv_share.astype(jnp.float32) * grad_scale,
        out_share.astype(jnp.float32) * grad_scale,
    )


def solution(mesh):
    placed = (P("lat", "lon", None), P(), P(), P(), P("lat", "lon", None))
    return jax.shard_map(
        shards,
        mesh=mesh,
        in_specs=placed,
        out_specs=(
            P("lat", "lon", None),
            P("lat", "lon", None),
            P(("lat", "lon"), None),
            P(("lat", "lon"), None),
        ),
        check_vma=False,
    )
```
